32 devices in a mesh: groups: 2 (over x), frames: 16 (over z, y, core).
Axes of the slice: x: 2, y: 2, z: 4, core: 2. Of those that a mesh axis runs over, the one named last changes fastest.
Arguments:
- latents: bfloat16 [4, 64, 128, 320], P('groups', 'frames'), parts along dimension 0, may hold values from -6 to 6
- in_weight: bfloat16 [3, 3, 320, 320], replicated, may hold values from -0.109375 to 0.109375
- time_weight: bfloat16 [3, 320, 320], replicated, may hold values from -0.1875 to 0.1875
- mid_weight: bfloat16 [3, 3, 320, 640], replicated, may hold values from -0.109375 to 0.109375
- up_weight: bfloat16 [3, 3, 960, 320], replicated, may hold values from -0.0625 to 0.0625
Outputs:
- mixed: bfloat16 [4, 64, 128, 320], P('groups', 'frames'), parts along dimension 0
The draws below stay inside these ranges and needn't reach their ends.
There are 2 independent parts, one for each index of `groups`. The reference program is written for one: setup_inputs(seed, part) draws one part's arguments, and reference() takes and returns one part's arrays. A program takes and returns all parts, laid end to end along the dimension named above; an argument that names none is the same for every part. Nothing has to cross between parts.
All inputs are finite; a program needn't handle non-finite values.
Results may differ from the reference program's by a relative error of at most 0.0045.
Values may be sent and summed in bfloat16 or wider, within the bound.
A program may use at most 64 MiB of HBM per device.

```python
import jax
import jax.numpy as jnp
from jax import lax

C = 320
CM = 640
W = 128
FRAMES = 4
CLIPS = 2
ROWS = 64


def steps_of(own_key, extent, cuts, smallest, largest):
    def one(axis_at, parts):
        steps = jax.random.uniform(jax.random.fold_in(jax.random.fold_in(own_key, 6), axis_at), (parts,), jnp.float32, smallest / len(cuts), largest / len(cuts))
        return jnp.repeat(jnp.exp(steps), extent[axis_at] // parts).reshape((-1,) + (1,) * (len(extent) - axis_at - 1))

    level = one(*cuts[0])
    for cut in cuts[1:]:
        level = level * one(*cut)
    return level


def scatter_about(key, dims, width, bound, shards=(), kind=jnp.bfloat16):
    level = steps_of(key, dims, shards, -0.22, 0.18) if shards else 1.0
    entries = jax.random.normal(key, dims, jnp.float32) * width * level
    return jnp.minimum(jnp.maximum(entries, -bound), bound).astype(kind)


def setup_inputs(seed: int = 0, part: int = 0) -> dict:
    key_list = jax.random.split(jax.random.key(seed), 6)
    part_keys = jax.random.split(jax.random.fold_in(key_list[5], part), 6)
    return {
        "latents": scatter_about(part_keys[0], (CLIPS, ROWS, W, C), 1.0, 6.0, ((1, 16),)),
        "in_weight": scatter_about(key_list[1], (3, 3, C, C), (9 * C) ** -0.5, 0.109375),
        "time_weight": scatter_about(key_list[2], (3, C, C), (3 * C) ** -0.5, 0.1875),
        "mid_weight": scatter_about(key_list[3], (3, 3, C, CM), (9 * C) ** -0.5, 0.109375),
        "up_weight": scatter_about(key_list[4], (3, 3, C + CM, C), (9 * (C + CM)) ** -0.5, 0.0625),
    }


def convolve(field, weight):
    return lax.conv_general_dilated(field.astype(jnp.float32), weight.astype(jnp.float32), (1, 1), ((1, 1), (1, 1)), dimension_numbers=("NHWC", "HWIO", "NHWC"), precision=lax.Precision.HIGHEST)


def reference(latents, in_weight, time_weight, mid_weight, up_weight):
    clip_count = latents.shape[0]
    height = latents.shape[1] // FRAMES
    columns = latents.shape[2]
    channels = latents.shape[3]
    offset = height // 2
    ordered = jnp.roll(latents, offset, axis=1)
    frames_all = ordered.reshape(clip_count * FRAMES, height, columns, channels)
    first = jax.nn.silu(convolve(frames_all, in_weight)).astype(jnp.bfloat16)
    series = first.reshape(clip_count, FRAMES, height * columns, channels).astype(jnp.float32)
    padded = jnp.pad(series, ((0, 0), (1, 1), (0, 0), (0, 0)))
    stacked = jnp.concatenate([padded[:, :-2], series, padded[:, 2:]], axis=-1)
    merged = time_weight.astype(jnp.float32).reshape(3 * channels, channels)
    temporal = jnp.einsum("abpk,kc->abpc", stacked, merged, precision=lax.Precision.HIGHEST)
    skip = (series + temporal).astype(jnp.bfloat16).reshape(clip_count * FRAMES, height, columns, channels)
    pooled = skip.astype(jnp.float32).reshape(clip_count * FRAMES, height // 2, 2, columns // 2, 2, channels).mean(axis=(2, 4)).astype(jnp.bfloat16)
    middle = jax.nn.silu(convolve(pooled, mid_weight)).astype(jnp.bfloat16)
    upper = jnp.repeat(jnp.repeat(middle, 2, axis=1), 2, axis=2)
    joined = jnp.concatenate([skip, upper], axis=-1)
    mixed = (frames_all.astype(jnp.float32) + convolve(joined, up_weight)).astype(jnp.bfloat16)
    return jnp.roll(mixed.reshape(latents.shape), -offset, axis=1)
```

```python
import functools

import jax
import jax.numpy as jnp
from jax import lax
from jax.experimental import pallas as pl
from jax.experimental.pallas import tpu as pltpu
from jax.sharding import PartitionSpec as P

FRAMES = 4
MESH = pl.DeviceIdType.MESH
F32 = jnp.float32
BF16 = jnp.bfloat16


def mm(a, b):
    return jnp.dot(a, b, preferred_element_type=F32)


def later(v):
    at = lax.broadcasted_iota(jnp.int32, v.shape, 0)
    return jnp.where(at == 0, 0.0, pltpu.roll(v, 1, 0))


def sooner(v):
    at = lax.broadcasted_iota(jnp.int32, v.shape, 0)
    return jnp.where(at == v.shape[0] - 1, 0.0, pltpu.roll(v, v.shape[0] - 1, 0))


def silu(v):
    return v / (1.0 + jnp.exp(-v))


def kernel(
    count, x_hbm, in_hbm, time_hbm, mid_hbm, up_hbm, out_hbm,
    x3, s3, m3, win, wtime, wmid, wup, wskip, wpool, raw, raw_got, base, mine, got, edge,
    edge_got, middle, mid_acc, acc, out_v, passing,
    w_sem, x_sem, o_sem, h_send, h_recv, t_send, t_recv, e_send, e_recv, r_send, r_recv,
):
    clips, rows, c, columns = x_hbm.shape
    half, double = columns // 2, 2 * c
    pooled_rows = rows // 2
    bands = count // FRAMES
    idx = lax.axis_index("frames")
    placed = lax.rem(idx + bands // 2, count)
    band = lax.rem(placed, bands)
    frame = placed // bands
    has = {
        "up": band > 0,
        "down": band < bands - 1,
        "prev": frame > 0,
        "next": frame < FRAMES - 1,
    }
    who = {
        "up": lax.rem(idx + count - 1, count),
        "down": lax.rem(idx + 1, count),
        "prev": lax.rem(idx + count - bands, count),
        "next": lax.rem(idx + bands, count),
    }

    reach = bands // 2
    detour = bands == 4
    ends = jnp.logical_and(frame < 2, band < reach)
    first_hop = jnp.logical_and(frame == FRAMES - 1, band >= reach)
    last_hop = jnp.logical_and(frame == 0, band >= reach)
    hops = jnp.logical_or(first_hop, last_hop)
    far_next = jnp.logical_and(frame == 0, band < reach)
    far_prev = jnp.logical_and(frame == 1, band < reach)
    greet = [(has[name], who[name]) for name in has]
    if detour:
        who["relay"] = lax.rem(idx + count - reach, count)
        who["end"] = lax.rem(idx + reach, count)
        who["over"] = jnp.where(
            first_hop, lax.rem(idx + 2 * reach, count), lax.rem(idx + count - 2 * reach, count))
        greet += [(ends, who["relay"]), (hops, who["end"]), (hops, who["over"])]

    def remote(src, dst, send, recv, name):
        return pltpu.make_async_remote_copy(
            src_ref=src, dst_ref=dst, send_sem=send, recv_sem=recv,
            device_id={"frames": who[name]}, device_id_type=MESH,
        )

    def start(copy, name):
        @pl.when(has[name])
        def _():
            copy.start()

    def landed(copy, name):
        @pl.when(has[name])
        def _():
            copy.wait_recv()

    sent = []

    loads = []
    for k in range(clips):
        loads.append(pltpu.make_async_copy(
            x_hbm.at[k], raw.at[k], x_sem.at[k]))
        loads[-1].start()
    weights = []
    for n, (src, dst) in enumerate(((in_hbm, win), (time_hbm, wtime), (mid_hbm, wmid), (up_hbm, wup))):
        weights.append(pltpu.make_async_copy(src, dst, w_sem.at[n]))
        weights[-1].start()

    barrier = pltpu.get_barrier_semaphore()
    for there, target in greet:
        @pl.when(there)
        def _(target=target):
            pl.semaphore_signal(
                barrier, inc=1, device_id={"frames": target}, device_id_type=MESH)
    pl.semaphore_wait(barrier, sum(there.astype(jnp.int32) for there, _ in greet))

    halo = {}
    for k in range(clips):
        for side, (to, row) in enumerate((("down", rows - 1), ("up", 0))):
            copy = remote(
                x_hbm.at[k, row], raw_got.at[k, side],
                h_send.at[k, side], h_recv.at[k, side], to)
            start(copy, to)
            halo[k, side] = copy
            sent.append((copy, to))
    sources = ("up", "down")
    steps = ("prev", "next")

    for side in range(2):
        @pl.when(jnp.logical_not(has[sources[side]]))
        def _(side=side):
            for k in range(clips):
                raw_got[k, side] = jnp.zeros((c, columns), BF16)
                edge_got[k, side] = jnp.zeros(edge_got.shape[2:], BF16)
        @pl.when(jnp.logical_not(has[steps[side]]))
        def _(side=side):
            for k in range(clips):
                got[k, side] = jnp.zeros(got.shape[2:], BF16)

    at = lax.broadcasted_iota(jnp.int32, (columns, columns), 0)
    to = lax.broadcasted_iota(jnp.int32, (columns, columns), 1)
    source = jnp.where(at < half, 2 * at, 2 * (at - half) + 1)
    split = jnp.where(to == source, 1.0, 0.0).astype(BF16)

    def place(k, slot, stored):
        value = lax.dot_general(
            split, stored, (((1,), (1,)), ((), ())), preferred_element_type=F32).astype(BF16)
        x3[k, slot, half:, :double] = jnp.concatenate([value[:half], value[half:]], axis=1)
        widen(x3, k, slot)

    def widen(dst, k, slot):
        row = dst[k, slot, half:, :double]
        even, odd = row[:, :c], row[:, c:]
        dst[k, slot, half:, double:] = sooner(even.astype(F32)).astype(BF16)
        dst[k, slot, :half, :] = jnp.concatenate(
            [later(odd.astype(F32)).astype(BF16), even, odd], axis=1)

    inner = list(range(1, rows - 1))
    order = inner + [0, rows - 1]
    parts = ((0, len(inner)), (len(inner), 2))

    def conv(src, k, picked, wref):
        total = None
        for dr in range(3):
            lhs = jnp.concatenate([src[k, r + dr] for r in picked], axis=0)
            term = mm(lhs, wref[dr].reshape(3 * c, c))
            total = term if total is None else total + term
        return total

    times = {}

    def first_part(k, part):
        at, size = parts[part]
        picked = order[at:at + size]
        value = silu(conv(x3, k, picked, win)).astype(BF16)
        for j in range(size):
            lo = 2 * half * j
            mine[k, at + j] = jnp.concatenate(
                [value[lo:lo + half], value[lo + half:lo + 2 * half]], axis=1)
        for side, to in ((0, "next"), (1, "prev")):
            copy = remote(
                mine.at[k, pl.ds(at, size)], got.at[k, side, pl.ds(at, size)],
                t_send.at[k, part, side], t_recv.at[k, part, side], to)
            if detour and part == 0:
                far = (far_next, far_prev)[side]
                by = remote(
                    mine.at[k, pl.ds(at, size)], passing.at[side, k],
                    t_send.at[k, part, side], r_recv.at[side, k], "relay")
                @pl.when(far)
                def _(by=by):
                    by.start()
                @pl.when(jnp.logical_and(has[to], jnp.logical_not(far)))
                def _(copy=copy):
                    copy.start()
            else:
                start(copy, to)
            times[k, part, side] = copy
            sent.append((copy, to))

    def over(flow, k):
        return remote(
            passing.at[flow, k], passing.at[flow, k],
            r_send.at[flow, k], r_recv.at[flow, k], "over")

    def home(flow, k):
        size = parts[0][1]
        return remote(
            passing.at[flow, k], got.at[k, flow, pl.ds(0, size)],
            r_send.at[flow, k], t_recv.at[k, 0, flow], "end")

    def pass_on(made, one, other):
        if not detour:
            return
        for k in range(clips):
            for there, flow in ((one, 0), (other, 1)):
                @pl.when(there)
                def _(flow=flow, k=k):
                    copy = made(flow, k)
                    over(flow, k).wait_recv()
                    copy.start()

    def stack(ref_value, size):
        v = ref_value.reshape(size * half, double)
        return jnp.concatenate([v[:, :c], v[:, c:]], axis=0)

    def own_part(k, part):
        at, size = parts[part]
        own = stack(mine[k, at:at + size], size)
        total = own.astype(F32) + mm(own, wtime[1])
        base[k, at:at + size] = total.reshape(size, columns, c)

    def skip_part(k, part):
        at, size = parts[part]
        total = base[k, at:at + size].reshape(size * columns, c)
        for side in range(2):
            landed(times[k, part, side], steps[side])
            total = total + mm(stack(got[k, side, at:at + size], size), wtime[2 * side])
        value = total.astype(BF16)
        n = size * half
        for j in range(size):
            s3[k, order[at + j] + 1, half:, :double] = jnp.concatenate(
                [value[j * half:(j + 1) * half], value[n + j * half:n + (j + 1) * half]], axis=1)

    edges = {}

    def share(k):
        pools = []
        for p in range(pooled_rows):
            pair = (s3[k, 2 * p + 1, half:, :double].astype(F32)
                    + s3[k, 2 * p + 2, half:, :double].astype(F32))
            pools.append(((pair[:, :c] + pair[:, c:]) * 0.25).astype(BF16))
        for side, (to, row, near) in enumerate((
            ("down", rows, pools[-2:]), ("up", 1, pools[:2]))):
            edge[k, side, 0] = s3[k, row, half:, :double]
            edge[k, side, 1] = jnp.concatenate(near, axis=1)
        for item in (1, 0):
            for side, to in enumerate(("down", "up")):
                copy = remote(
                    edge.at[k, side, item], edge_got.at[k, side, item],
                    e_send.at[k, side, item], e_recv.at[k, side, item], to)
                start(copy, to)
                edges[k, side, item] = copy
                sent.append((copy, to))
        for p in range(pooled_rows):
            spread(k, p + 2, pools[p])

    def spread(k, slot, pool):
        wide = pool.astype(F32)
        m3[k, slot] = jnp.concatenate(
            [later(wide).astype(BF16), pool, sooner(wide).astype(BF16)], axis=1)

    def turn_weights():
        for dr in range(3):
            turned = wup[dr].reshape(3 * c, -1).T
            wpool[dr] = turned[c:]
            for dw in range(3):
                wskip[dr, dw * c:(dw + 1) * c] = turned[:c, dw * c:(dw + 1) * c]

    def skip_weight(dr):
        return wskip[dr]

    wide = 2 * half

    def mid_weight(dr):
        return wmid[dr].reshape(3 * c, -1)

    def mid_inner(k):
        local = m3[k, 2:pooled_rows + 2].reshape(pooled_rows * half, 3 * c)
        mid_acc[k] = jnp.zeros(mid_acc.shape[1:], F32)
        for dr in range(3):
            term = mm(local, mid_weight(dr))
            mid_acc[k, 2 - dr:2 - dr + pooled_rows] += term.reshape(pooled_rows, half, -1)

    def up_inner(k):
        for r in range(rows):
            widen(s3, k, r + 1)
        centre = mm(s3[k, 1:rows + 1].reshape(rows * wide, 3 * c), skip_weight(1))
        acc[k] = centre.reshape(rows, wide, c)
        n = rows - 1
        lower = mm(s3[k, 1:rows].reshape(n * wide, 3 * c), skip_weight(0))
        acc[k, 1:rows] += lower.reshape(n, wide, c)
        upper = mm(s3[k, 2:rows + 1].reshape(n * wide, 3 * c), skip_weight(2))
        acc[k, :n] += upper.reshape(n, wide, c)

    def finish(k):
        for side in range(2):
            landed(edges[k, side, 1], sources[side])
            both = edge_got[k, side, 1]
            first_slot = (0, pooled_rows + 2)[side]
            spread(k, first_slot, both[:, :c])
            spread(k, first_slot + 1, both[:, c:])
        n = pooled_rows + 2
        mid_acc[k, :2] += mm(
            m3[k, :2].reshape(2 * half, 3 * c), mid_weight(0)).reshape(2, half, -1)
        mid_acc[k, n - 2:] += mm(
            m3[k, n:].reshape(2 * half, 3 * c), mid_weight(2)).reshape(2, half, -1)
        term = mm(jnp.concatenate([m3[k, 1], m3[k, n]], axis=0), mid_weight(1))
        mid_acc[k, 0] += term[:half]
        mid_acc[k, n - 1] += term[half:]
        total = mid_acc[k]
        value = silu(total).astype(BF16)
        middle[k] = value
        @pl.when(jnp.logical_not(has["up"]))
        def _():
            middle[k, 0] = jnp.zeros(middle.shape[2:], BF16)
        @pl.when(jnp.logical_not(has["down"]))
        def _():
            middle[k, n - 1] = jnp.zeros(middle.shape[2:], BF16)
        for side in range(2):
            landed(edges[k, side, 0], sources[side])
            slot = (0, rows + 1)[side]
            s3[k, slot, half:, :double] = edge_got[k, side, 0]
            widen(s3, k, slot)
        acc[k, 0] += mm(s3[k, 0], skip_weight(0))
        acc[k, rows - 1] += mm(s3[k, rows + 1], skip_weight(2))
        spans = ((0, n - 1), (1, n - 2), (1, n - 1))
        terms = {}
        for dr, (at, size) in enumerate(spans):
            lhs = middle[k, at:at + size].reshape(size * half, -1)
            term = mm(lhs, wpool[dr])
            for j in range(size):
                terms[dr, at + j] = term[j * half:(j + 1) * half]
        for r in range(rows):
            taps = sum(terms[dr, (r + dr + 1) // 2] for dr in range(3))
            cols = [taps[:, dw * c:(dw + 1) * c] for dw in range(3)]
            even = later(cols[0]) + cols[1] + cols[2] + acc[k, r, :half]
            odd = cols[0] + cols[1] + sooner(cols[2]) + acc[k, r, half:]
            own = x3[k, r + 1, half:, :double].astype(F32)
            value = jnp.concatenate([even + own[:, :c], odd + own[:, c:]], axis=0).astype(BF16)
            out_hbm[k, r] = mm(value.T, split).astype(BF16)
        return None

    weights[0].wait()
    for k in range(clips):
        loads[k].wait()
        for r in range(rows):
            place(k, r + 1, raw[k, r])
        first_part(k, 0)
    pass_on(over, first_hop, last_hop)
    for k in range(clips):
        for side in range(2):
            landed(halo[k, side], sources[side])
            place(k, (0, rows + 1)[side], raw_got[k, side])
        first_part(k, 1)
    for one in weights[1:]:
        one.wait()
    for k in range(clips):
        own_part(k, 0)
        own_part(k, 1)
    turn_weights()
    pass_on(home, last_hop, first_hop)
    outs = []
    for k in range(clips):
        skip_part(k, 0)
        skip_part(k, 1)
        share(k)
        if k > 0:
            outs.append(finish(k - 1))
        mid_inner(k)
        up_inner(k)
    outs.append(finish(clips - 1))
    if detour:
        for flow in range(2):
            @pl.when(hops)
            def _(flow=flow):
                for k in range(clips):
                    over(flow, k).wait_send()
    for copy, to in sent:
        @pl.when(has[to])
        def _(copy=copy):
            copy.wait_send()


def body(count, latents, in_weight, time_weight, mid_weight, up_weight):
    clips, rows, columns, c = latents.shape
    cm = mid_weight.shape[-1]
    half, double = columns // 2, 2 * c
    flat = latents.swapaxes(2, 3)
    up_stored = up_weight.swapaxes(2, 3)
    dma = pltpu.SemaphoreType.DMA
    vmem = lambda *shape: pltpu.VMEM(shape, BF16)
    hbm = pl.BlockSpec(memory_space=pl.ANY)
    out = pl.pallas_call(
        functools.partial(kernel, count),
        out_shape=pltpu.VMEM(flat.shape, BF16),
        in_specs=[hbm] * 5,
        out_specs=pl.BlockSpec(memory_space=pltpu.VMEM),
        scratch_shapes=[
            vmem(clips, rows + 2, 2 * half, 3 * c),
            vmem(clips, rows + 2, 2 * half, 3 * c),
            vmem(clips, rows // 2 + 4, half, 3 * c),
            vmem(*in_weight.shape), vmem(*time_weight.shape),
            vmem(*mid_weight.shape), vmem(*up_stored.shape),
            vmem(3, 3 * c, c), vmem(3, cm, 3 * c),
            vmem(clips, rows, c, columns), vmem(clips, 2, c, columns),
            pltpu.VMEM((clips, rows, columns, c), F32),
            vmem(clips, rows, half, double),
            vmem(clips, 2, rows, half, double),
            vmem(clips, 2, 2, half, double),
            vmem(clips, 2, 2, half, double),
            vmem(clips, rows // 2 + 2, half, cm),
            pltpu.VMEM((clips, rows // 2 + 2, half, cm), F32),
            pltpu.VMEM((clips, rows, 2 * half, c), F32),
            vmem(clips, rows, c, columns), vmem(2, clips, rows - 2, half, double),
            dma((4,)), dma((clips,)), dma((clips,)),
            dma((clips, 2)), dma((clips, 2)),
            dma((clips, 2, 2)), dma((clips, 2, 2)),
            dma((clips, 2, 2)), dma((clips, 2, 2)),
            dma((2, clips)), dma((2, clips)),
        ],
        compiler_params=pltpu.CompilerParams(
            collective_id=0, has_side_effects=True, vmem_limit_bytes=50 * 1024 * 1024),
    )(*[pltpu.with_memory_space_constraint(v, pltpu.HBM) for v in (flat, in_weight, time_weight, mid_weight, up_stored)])
    return out.swapaxes(2, 3)


def solution(mesh):
    in_specs = (P("groups", "frames", None, None), P(), P(), P(), P())
    out_specs = P("groups", "frames", None, None)
    return jax.shard_map(
        functools.partial(body, mesh.shape["frames"]),
        mesh=mesh, in_specs=in_specs, out_specs=out_specs, check_vma=False)
```

```python
import functools

import jax
import jax.numpy as jnp
from jax import lax
from jax.experimental import pallas as pl
from jax.experimental.pallas import tpu as pltpu
from jax.sharding import PartitionSpec as P

FRAMES = 4
MESH = pl.DeviceIdType.MESH
F32 = jnp.float32
BF16 = jnp.bfloat16


def mm(a, b):
    return jnp.dot(a, b, preferred_element_type=F32)


def later(v):
    at = lax.broadcasted_iota(jnp.int32, v.shape, 0)
    return jnp.where(at == 0, 0.0, pltpu.roll(v, 1, 0))


def sooner(v):
    at = lax.broadcasted_iota(jnp.int32, v.shape, 0)
    return jnp.where(at == v.shape[0] - 1, 0.0, pltpu.roll(v, v.shape[0] - 1, 0))


def silu(v):
    return v / (1.0 + jnp.exp(-v))


def kernel(
    count, x_hbm, in_hbm, time_hbm, mid_hbm, up_hbm, out_hbm,
    x3, s3, m3, win, wtime, wmid, wup, wskip, wpool, raw, raw_got, base, mine, got, edge,
    edge_got, middle, mid_acc, acc, out_v, passing,
    w_sem, x_sem, o_sem, h_send, h_recv, t_send, t_recv, e_send, e_recv, r_send, r_recv,
):
    clips, rows, c, columns = x_hbm.shape
    half, double = columns // 2, 2 * c
    pooled_rows = rows // 2
    bands = count // FRAMES
    idx = lax.axis_index("frames")
    placed = lax.rem(idx + bands // 2, count)
    band = lax.rem(placed, bands)
    frame = placed // bands
    has = {
        "up": band > 0,
        "down": band < bands - 1,
        "prev": frame > 0,
        "next": frame < FRAMES - 1,
    }
    who = {
        "up": lax.rem(idx + count - 1, count),
        "down": lax.rem(idx + 1, count),
        "prev": lax.rem(idx + count - bands, count),
        "next": lax.rem(idx + bands, count),
    }

    reach = bands // 2
    detour = bands == 4
    ends = jnp.logical_and(frame < 2, band < reach)
    first_hop = jnp.logical_and(frame == FRAMES - 1, band >= reach)
    last_hop = jnp.logical_and(frame == 0, band >= reach)
    hops = jnp.logical_or(first_hop, last_hop)
    far_next = jnp.logical_and(frame == 0, band < reach)
    far_prev = jnp.logical_and(frame == 1, band < reach)
    greet = [(has[name], who[name]) for name in has]
    if detour:
        who["relay"] = lax.rem(idx + count - reach, count)
        who["end"] = lax.rem(idx + reach, count)
        who["over"] = jnp.where(
            first_hop, lax.rem(idx + 2 * reach, count), lax.rem(idx + count - 2 * reach, count))
        greet += [(ends, who["relay"]), (hops, who["end"]), (hops, who["over"])]

    def remote(src, dst, send, recv, name):
        return pltpu.make_async_remote_copy(
            src_ref=src, dst_ref=dst, send_sem=send, recv_sem=recv,
            device_id={"frames": who[name]}, device_id_type=MESH,
        )

    def start(copy, name):
        @pl.when(has[name])
        def _():
            copy.start()

    def landed(copy, name):
        @pl.when(has[name])
        def _():
            copy.wait_recv()

    sent = []

    loads = []
    for k in range(clips):
        loads.append(pltpu.make_async_copy(
            x_hbm.at[k], raw.at[k], x_sem.at[k]))
        loads[-1].start()
    weights = []
    for n, (src, dst) in enumerate(((in_hbm, win), (time_hbm, wtime), (mid_hbm, wmid), (up_hbm, wup))):
        weights.append(pltpu.make_async_copy(src, dst, w_sem.at[n]))
        weights[-1].start()

    barrier = pltpu.get_barrier_semaphore()
    for there, target in greet:
        @pl.when(there)
        def _(target=target):
            pl.semaphore_signal(
                barrier, inc=1, device_id={"frames": target}, device_id_type=MESH)
    pl.semaphore_wait(barrier, sum(there.astype(jnp.int32) for there, _ in greet))

    halo = {}
    for k in range(clips):
        for side, (to, row) in enumerate((("down", rows - 1), ("up", 0))):
            copy = remote(
                x_hbm.at[k, row], raw_got.at[k, side],
                h_send.at[k, side], h_recv.at[k, side], to)
            start(copy, to)
            halo[k, side] = copy
            sent.append((copy, to))
    sources = ("up", "down")
    steps = ("prev", "next")

    for side in range(2):
        @pl.when(jnp.logical_not(has[sources[side]]))
        def _(side=side):
            for k in range(clips):
                raw_got[k, side] = jnp.zeros((c, columns), BF16)
                edge_got[k, side] = jnp.zeros(edge_got.shape[2:], BF16)
        @pl.when(jnp.logical_not(has[steps[side]]))
        def _(side=side):
            for k in range(clips):
                got[k, side] = jnp.zeros(got.shape[2:], BF16)

    at = lax.broadcasted_iota(jnp.int32, (columns, columns), 0)
    to = lax.broadcasted_iota(jnp.int32, (columns, columns), 1)
    source = jnp.where(at < half, 2 * at, 2 * (at - half) + 1)
    split = jnp.where(to == source, 1.0, 0.0).astype(BF16)

    def place(k, slot, stored):
        value = lax.dot_general(
            split, stored, (((1,), (1,)), ((), ())), preferred_element_type=F32).astype(BF16)
        x3[k, slot, half:, :double] = jnp.concatenate([value[:half], value[half:]], axis=1)
        widen(x3, k, slot)

    def widen(dst, k, slot):
        row = dst[k, slot, half:, :double]
        even, odd = row[:, :c], row[:, c:]
        dst[k, slot, half:, double:] = sooner(even.astype(F32)).astype(BF16)
        dst[k, slot, :half, :] = jnp.concatenate(
            [later(odd.astype(F32)).astype(BF16), even, odd], axis=1)

    inner = list(range(1, rows - 1))
    order = inner + [0, rows - 1]
    parts = ((0, len(inner)), (len(inner), 2))

    def conv(src, k, picked, wref):
        total = None
        for dr in range(3):
            lhs = jnp.concatenate([src[k, r + dr] for r in picked], axis=0)
            term = mm(lhs, wref[dr].reshape(3 * c, c))
            total = term if total is None else total + term
        return total

    times = {}

    def first_part(k, part):
        at, size = parts[part]
        picked = order[at:at + size]
        value = silu(conv(x3, k, picked, win)).astype(BF16)
        for j in range(size):
            lo = 2 * half * j
            mine[k, at + j] = jnp.concatenate(
                [value[lo:lo + half], value[lo + half:lo + 2 * half]], axis=1)

    outer = jnp.logical_or(band == 0, band == bands - 1)
    inside = jnp.logical_not(outer)

    def send_part(k, part, now=None, way=None):
        at, size = parts[part]
        gate = lambda there: there if now is None else jnp.logical_and(there, now)
        for side, to in ((0, "next"), (1, "prev")):
            if way is not None:
                distant = (far_next, far_prev)[side]
                mask = distant if way == "far" else jnp.logical_not(distant)
                gate = lambda there, mask=mask: jnp.logical_and(
                    there if now is None else jnp.logical_and(there, now), mask)
            copy = remote(
                mine.at[k, pl.ds(at, size)], got.at[k, side, pl.ds(at, size)],
                t_send.at[k, part, side], t_recv.at[k, part, side], to)
            if detour and part == 0:
                far = (far_next, far_prev)[side]
                by = remote(
                    mine.at[k, pl.ds(at, size)], passing.at[side, k],
                    t_send.at[k, part, side], r_recv.at[side, k], "relay")
                @pl.when(gate(far))
                def _(by=by):
                    by.start()
                @pl.when(gate(jnp.logical_and(has[to], jnp.logical_not(far))))
                def _(copy=copy):
                    copy.start()
            else:
                @pl.when(gate(has[to]))
                def _(copy=copy):
                    copy.start()
            if (k, part, side) not in times:
                times[k, part, side] = copy
                sent.append((copy, to))

    def over(flow, k):
        return remote(
            passing.at[flow, k], passing.at[flow, k],
            r_send.at[flow, k], r_recv.at[flow, k], "over")

    def home(flow, k):
        size = parts[0][1]
        return remote(
            passing.at[flow, k], got.at[k, flow, pl.ds(0, size)],
            r_send.at[flow, k], t_recv.at[k, 0, flow], "end")

    def pass_on(made, one, other, picked):
        if not detour:
            return
        for k in picked:
            for there, flow in ((one, 0), (other, 1)):
                @pl.when(there)
                def _(flow=flow, k=k):
                    copy = made(flow, k)
                    over(flow, k).wait_recv()
                    copy.start()

    def stack(ref_value, size):
        v = ref_value.reshape(size * half, double)
        return jnp.concatenate([v[:, :c], v[:, c:]], axis=0)

    def own_part(k, part):
        at, size = parts[part]
        own = stack(mine[k, at:at + size], size)
        total = own.astype(F32) + mm(own, wtime[1])
        base[k, at:at + size] = total.reshape(size, columns, c)

    def skip_part(k, part):
        at, size = parts[part]
        total = base[k, at:at + size].reshape(size * columns, c)
        for side in range(2):
            landed(times[k, part, side], steps[side])
            total = total + mm(stack(got[k, side, at:at + size], size), wtime[2 * side])
        value = total.astype(BF16)
        n = size * half
        for j in range(size):
            s3[k, order[at + j] + 1, half:, :double] = jnp.concatenate(
                [value[j * half:(j + 1) * half], value[n + j * half:n + (j + 1) * half]], axis=1)

    edges = {}

    def share(k):
        pools = []
        for p in range(pooled_rows):
            pair = (s3[k, 2 * p + 1, half:, :double].astype(F32)
                    + s3[k, 2 * p + 2, half:, :double].astype(F32))
            pools.append(((pair[:, :c] + pair[:, c:]) * 0.25).astype(BF16))
        for side, (to, row, near) in enumerate((
            ("down", rows, pools[-2:]), ("up", 1, pools[:2]))):
            edge[k, side, 0] = s3[k, row, half:, :double]
            edge[k, side, 1] = jnp.concatenate(near, axis=1)
        for item in (1, 0):
            for side, to in enumerate(("down", "up")):
                copy = remote(
                    edge.at[k, side, item], edge_got.at[k, side, item],
                    e_send.at[k, side, item], e_recv.at[k, side, item], to)
                start(copy, to)
                edges[k, side, item] = copy
                sent.append((copy, to))
        for p in range(pooled_rows):
            spread(k, p + 2, pools[p])

    def spread(k, slot, pool):
        wide = pool.astype(F32)
        m3[k, slot] = jnp.concatenate(
            [later(wide).astype(BF16), pool, sooner(wide).astype(BF16)], axis=1)

    def turn_weights():
        for dr in range(3):
            turned = wup[dr].reshape(3 * c, -1).T
            wpool[dr] = turned[c:]
            for dw in range(3):
                wskip[dr, dw * c:(dw + 1) * c] = turned[:c, dw * c:(dw + 1) * c]

    def skip_weight(dr):
        return wskip[dr]

    wide = 2 * half

    def mid_weight(dr):
        return wmid[dr].reshape(3 * c, -1)

    def mid_inner(k):
        local = m3[k, 2:pooled_rows + 2].reshape(pooled_rows * half, 3 * c)
        mid_acc[k] = jnp.zeros(mid_acc.shape[1:], F32)
        for dr in range(3):
            term = mm(local, mid_weight(dr))
            mid_acc[k, 2 - dr:2 - dr + pooled_rows] += term.reshape(pooled_rows, half, -1)

    def up_first(k):
        n = rows - 2
        for r in range(1, rows - 1):
            widen(s3, k, r + 1)
        lhs = s3[k, 2:rows].reshape(n * wide, 3 * c)
        acc[k, 1:rows - 1] = mm(lhs, skip_weight(1)).reshape(n, wide, c)
        lower = mm(lhs, skip_weight(0)).reshape(n, wide, c)
        acc[k, rows - 1] = lower[n - 1]
        if n > 1:
            acc[k, 2:rows - 1] += lower[:n - 1]
        upper = mm(lhs, skip_weight(2)).reshape(n, wide, c)
        acc[k, 0] = upper[0]
        if n > 1:
            acc[k, 1:rows - 2] += upper[1:]

    def up_second(k):
        for r in (0, rows - 1):
            widen(s3, k, r + 1)
        lhs = jnp.concatenate([s3[k, 1], s3[k, rows]], axis=0)
        centre = mm(lhs, skip_weight(1))
        acc[k, 0] += centre[:wide]
        acc[k, rows - 1] += centre[wide:]
        acc[k, 1] += mm(s3[k, 1], skip_weight(0))
        acc[k, rows - 2] += mm(s3[k, rows], skip_weight(2))

    def finish(k):
        for side in range(2):
            landed(edges[k, side, 1], sources[side])
            both = edge_got[k, side, 1]
            first_slot = (0, pooled_rows + 2)[side]
            spread(k, first_slot, both[:, :c])
            spread(k, first_slot + 1, both[:, c:])
        n = pooled_rows + 2
        mid_acc[k, :2] += mm(
            m3[k, :2].reshape(2 * half, 3 * c), mid_weight(0)).reshape(2, half, -1)
        mid_acc[k, n - 2:] += mm(
            m3[k, n:].reshape(2 * half, 3 * c), mid_weight(2)).reshape(2, half, -1)
        term = mm(jnp.concatenate([m3[k, 1], m3[k, n]], axis=0), mid_weight(1))
        mid_acc[k, 0] += term[:half]
        mid_acc[k, n - 1] += term[half:]
        total = mid_acc[k]
        value = silu(total).astype(BF16)
        middle[k] = value
        @pl.when(jnp.logical_not(has["up"]))
        def _():
            middle[k, 0] = jnp.zeros(middle.shape[2:], BF16)
        @pl.when(jnp.logical_not(has["down"]))
        def _():
            middle[k, n - 1] = jnp.zeros(middle.shape[2:], BF16)
        for side in range(2):
            landed(edges[k, side, 0], sources[side])
            slot = (0, rows + 1)[side]
            s3[k, slot, half:, :double] = edge_got[k, side, 0]
            widen(s3, k, slot)
        acc[k, 0] += mm(s3[k, 0], skip_weight(0))
        acc[k, rows - 1] += mm(s3[k, rows + 1], skip_weight(2))
        spans = ((0, n - 1), (1, n - 2), (1, n - 1))
        terms = {}
        for dr, (at, size) in enumerate(spans):
            lhs = middle[k, at:at + size].reshape(size * half, -1)
            term = mm(lhs, wpool[dr])
            for j in range(size):
                terms[dr, at + j] = term[j * half:(j + 1) * half]
        for r in range(rows):
            taps = sum(terms[dr, (r + dr + 1) // 2] for dr in range(3))
            cols = [taps[:, dw * c:(dw + 1) * c] for dw in range(3)]
            even = later(cols[0]) + cols[1] + cols[2] + acc[k, r, :half]
            odd = cols[0] + cols[1] + sooner(cols[2]) + acc[k, r, half:]
            own = x3[k, r + 1, half:, :double].astype(F32)
            value = jnp.concatenate([even + own[:, :c], odd + own[:, c:]], axis=0).astype(BF16)
            out_hbm[k, r] = mm(value.T, split).astype(BF16)
        return None

    weights[0].wait()
    for k in range(clips):
        loads[k].wait()
        for r in range(rows):
            place(k, r + 1, raw[k, r])
        first_part(k, 0)
        send_part(k, 0, jnp.logical_not(hops) if detour and k > 0 else None)
    pass_on(over, first_hop, last_hop, range(clips))
    if detour:
        for k in range(1, clips):
            send_part(k, 0, hops)
    for k in range(clips):
        for side in range(2):
            landed(halo[k, side], sources[side])
            place(k, (0, rows + 1)[side], raw_got[k, side])
        first_part(k, 1)
        if detour:
            send_part(k, 1, None, "far")
            if k == clips - 1:
                for q in range(clips):
                    send_part(q, 1, inside, "near")
        else:
            send_part(k, 1)
    for one in weights[1:]:
        one.wait()
    for k in range(clips):
        own_part(k, 0)
        own_part(k, 1)
    turn_weights()
    pass_on(home, last_hop, first_hop, range(clips))
    for k in range(clips):
        if detour:
            send_part(k, 1, outer, "near")
    for k in range(clips):
        skip_part(k, 0)
        up_first(k)
        skip_part(k, 1)
        share(k)
        if k > 0:
            finish(k - 1)
        mid_inner(k)
        up_second(k)
    finish(clips - 1)
    if detour:
        for flow in range(2):
            @pl.when(hops)
            def _(flow=flow):
                for k in range(clips):
                    over(flow, k).wait_send()
    for copy, to in sent:
        @pl.when(has[to])
        def _(copy=copy):
            copy.wait_send()


def body(count, latents, in_weight, time_weight, mid_weight, up_weight):
    clips, rows, columns, c = latents.shape
    cm = mid_weight.shape[-1]
    half, double = columns // 2, 2 * c
    flat = latents.swapaxes(2, 3)
    up_stored = up_weight.swapaxes(2, 3)
    dma = pltpu.SemaphoreType.DMA
    vmem = lambda *shape: pltpu.VMEM(shape, BF16)
    hbm = pl.BlockSpec(memory_space=pl.ANY)
    out = pl.pallas_call(
        functools.partial(kernel, count),
        out_shape=pltpu.VMEM(flat.shape, BF16),
        in_specs=[hbm] * 5,
        out_specs=pl.BlockSpec(memory_space=pltpu.VMEM),
        scratch_shapes=[
            vmem(clips, rows + 2, 2 * half, 3 * c),
            vmem(clips, rows + 2, 2 * half, 3 * c),
            vmem(clips, rows // 2 + 4, half, 3 * c),
            vmem(*in_weight.shape), vmem(*time_weight.shape),
            vmem(*mid_weight.shape), vmem(*up_stored.shape),
            vmem(3, 3 * c, c), vmem(3, cm, 3 * c),
            vmem(clips, rows, c, columns), vmem(clips, 2, c, columns),
            pltpu.VMEM((clips, rows, columns, c), F32),
            vmem(clips, rows, half, double),
            vmem(clips, 2, rows, half, double),
            vmem(clips, 2, 2, half, double),
            vmem(clips, 2, 2, half, double),
            vmem(clips, rows // 2 + 2, half, cm),
            pltpu.VMEM((clips, rows // 2 + 2, half, cm), F32),
            pltpu.VMEM((clips, rows, 2 * half, c), F32),
            vmem(clips, rows, c, columns), vmem(2, clips, rows - 2, half, double),
            dma((4,)), dma((clips,)), dma((clips,)),
            dma((clips, 2)), dma((clips, 2)),
            dma((clips, 2, 2)), dma((clips, 2, 2)),
            dma((clips, 2, 2)), dma((clips, 2, 2)),
            dma((2, clips)), dma((2, clips)),
        ],
        compiler_params=pltpu.CompilerParams(
            collective_id=0, has_side_effects=True, vmem_limit_bytes=50 * 1024 * 1024),
    )(*[pltpu.with_memory_space_constraint(v, pltpu.HBM) for v in (flat, in_weight, time_weight, mid_weight, up_stored)])
    return out.swapaxes(2, 3)


def solution(mesh):
    in_specs = (P("groups", "frames", None, None), P(), P(), P(), P())
    out_specs = P("groups", "frames", None, None)
    return jax.shard_map(
        functools.partial(body, mesh.shape["frames"]),
        mesh=mesh, in_specs=in_specs, out_specs=out_specs, check_vma=False)
```

```python
import functools

import jax
import jax.numpy as jnp
from jax import lax
from jax.experimental import pallas as pl
from jax.experimental.pallas import tpu as pltpu
from jax.sharding import PartitionSpec as P

FRAMES = 4
MESH = pl.DeviceIdType.MESH
F32 = jnp.float32
BF16 = jnp.bfloat16


def mm(a, b):
    return jnp.dot(a, b, preferred_element_type=F32)


def later(v):
    at = lax.broadcasted_iota(jnp.int32, v.shape, 0)
    return jnp.where(at == 0, 0.0, pltpu.roll(v, 1, 0))


def sooner(v):
    at = lax.broadcasted_iota(jnp.int32, v.shape, 0)
    return jnp.where(at == v.shape[0] - 1, 0.0, pltpu.roll(v, v.shape[0] - 1, 0))


def silu(v):
    return v / (1.0 + jnp.exp(-v))


def kernel(
    count, x_hbm, in_hbm, time_hbm, mid_hbm, up_hbm, out_hbm,
    x3, s3, m3, win, wtime, wmid, wup, wskip, wpool, raw, raw_got, base, mine, got, edge,
    edge_got, middle, mid_acc, acc, out_v, passing,
    w_sem, x_sem, o_sem, h_send, h_recv, t_send, t_recv, e_send, e_recv, r_send, r_recv,
):
    clips, rows, c, columns = x_hbm.shape
    half, double = columns // 2, 2 * c
    pooled_rows = rows // 2
    bands = count // FRAMES
    idx = lax.axis_index("frames")
    placed = lax.rem(idx + bands // 2, count)
    band = lax.rem(placed, bands)
    frame = placed // bands
    has = {
        "up": band > 0,
        "down": band < bands - 1,
        "prev": frame > 0,
        "next": frame < FRAMES - 1,
    }
    who = {
        "up": lax.rem(idx + count - 1, count),
        "down": lax.rem(idx + 1, count),
        "prev": lax.rem(idx + count - bands, count),
        "next": lax.rem(idx + bands, count),
    }

    reach = bands // 2
    detour = bands == 4
    ends = jnp.logical_and(frame < 2, band < reach)
    first_hop = jnp.logical_and(frame == FRAMES - 1, band >= reach)
    last_hop = jnp.logical_and(frame == 0, band >= reach)
    hops = jnp.logical_or(first_hop, last_hop)
    far_next = jnp.logical_and(frame == 0, band < reach)
    far_prev = jnp.logical_and(frame == 1, band < reach)
    greet = [(has[name], who[name]) for name in has]
    if detour:
        who["relay"] = lax.rem(idx + count - reach, count)
        who["end"] = lax.rem(idx + reach, count)
        who["over"] = jnp.where(
            first_hop, lax.rem(idx + 2 * reach, count), lax.rem(idx + count - 2 * reach, count))
        greet += [(ends, who["relay"]), (hops, who["end"]), (hops, who["over"])]

    def remote(src, dst, send, recv, name):
        return pltpu.make_async_remote_copy(
            src_ref=src, dst_ref=dst, send_sem=send, recv_sem=recv,
            device_id={"frames": who[name]}, device_id_type=MESH,
        )

    def start(copy, name):
        @pl.when(has[name])
        def _():
            copy.start()

    def landed(copy, name):
        @pl.when(has[name])
        def _():
            copy.wait_recv()

    sent = []

    loads = []
    for k in range(clips):
        loads.append(pltpu.make_async_copy(
            x_hbm.at[k], raw.at[k], x_sem.at[k]))
        loads[-1].start()
    weights = []
    for n, (src, dst) in enumerate(((in_hbm, win), (time_hbm, wtime), (mid_hbm, wmid), (up_hbm, wup))):
        weights.append(pltpu.make_async_copy(src, dst, w_sem.at[n]))
        weights[-1].start()

    barrier = pltpu.get_barrier_semaphore()
    for there, target in greet:
        @pl.when(there)
        def _(target=target):
            pl.semaphore_signal(
                barrier, inc=1, device_id={"frames": target}, device_id_type=MESH)
    pl.semaphore_wait(barrier, sum(there.astype(jnp.int32) for there, _ in greet))

    halo = {}
    for k in range(clips):
        for side, (to, row) in enumerate((("down", rows - 1), ("up", 0))):
            copy = remote(
                x_hbm.at[k, row], raw_got.at[k, side],
                h_send.at[k, side], h_recv.at[k, side], to)
            start(copy, to)
            halo[k, side] = copy
            sent.append((copy, to))
    sources = ("up", "down")
    steps = ("prev", "next")

    for side in range(2):
        @pl.when(jnp.logical_not(has[sources[side]]))
        def _(side=side):
            for k in range(clips):
                raw_got[k, side] = jnp.zeros((c, columns), BF16)
                edge_got[k, side] = jnp.zeros(edge_got.shape[2:], BF16)
        @pl.when(jnp.logical_not(has[steps[side]]))
        def _(side=side):
            for k in range(clips):
                got[k, side] = jnp.zeros(got.shape[2:], BF16)

    at = lax.broadcasted_iota(jnp.int32, (columns, columns), 0)
    to = lax.broadcasted_iota(jnp.int32, (columns, columns), 1)
    source = jnp.where(at < half, 2 * at, 2 * (at - half) + 1)
    split = jnp.where(to == source, 1.0, 0.0).astype(BF16)

    def place(k, slot, stored):
        value = lax.dot_general(
            split, stored, (((1,), (1,)), ((), ())), preferred_element_type=F32).astype(BF16)
        x3[k, slot, half:, :double] = jnp.concatenate([value[:half], value[half:]], axis=1)
        widen(x3, k, slot)

    def widen(dst, k, slot):
        row = dst[k, slot, half:, :double]
        even, odd = row[:, :c], row[:, c:]
        dst[k, slot, half:, double:] = sooner(even.astype(F32)).astype(BF16)
        dst[k, slot, :half, :] = jnp.concatenate(
            [later(odd.astype(F32)).astype(BF16), even, odd], axis=1)

    inner = list(range(1, rows - 1))
    order = inner + [0, rows - 1]
    parts = ((0, len(inner)), (len(inner), 2))

    def conv(src, k, picked, wref):
        total = None
        for dr in range(3):
            lhs = jnp.concatenate([src[k, r + dr] for r in picked], axis=0)
            term = mm(lhs, wref[dr].reshape(3 * c, c))
            total = term if total is None else total + term
        return total

    times = {}

    def first_part(k, part):
        at, size = parts[part]
        picked = order[at:at + size]
        value = silu(conv(x3, k, picked, win)).astype(BF16)
        for j in range(size):
            lo = 2 * half * j
            mine[k, at + j] = jnp.concatenate(
                [value[lo:lo + half], value[lo + half:lo + 2 * half]], axis=1)

    outer = jnp.logical_or(band == 0, band == bands - 1)
    inside = jnp.logical_not(outer)

    def send_part(k, part, now=None, way=None):
        at, size = parts[part]
        gate = lambda there: there if now is None else jnp.logical_and(there, now)
        for side, to in ((0, "next"), (1, "prev")):
            if way is not None:
                distant = (far_next, far_prev)[side]
                mask = distant if way == "far" else jnp.logical_not(distant)
                gate = lambda there, mask=mask: jnp.logical_and(
                    there if now is None else jnp.logical_and(there, now), mask)
            copy = remote(
                mine.at[k, pl.ds(at, size)], got.at[k, side, pl.ds(at, size)],
                t_send.at[k, part, side], t_recv.at[k, part, side], to)
            if detour and part == 0:
                far = (far_next, far_prev)[side]
                by = remote(
                    mine.at[k, pl.ds(at, size)], passing.at[side, k],
                    t_send.at[k, part, side], r_recv.at[side, k], "relay")
                @pl.when(gate(far))
                def _(by=by):
                    by.start()
                @pl.when(gate(jnp.logical_and(has[to], jnp.logical_not(far))))
                def _(copy=copy):
                    copy.start()
            else:
                @pl.when(gate(has[to]))
                def _(copy=copy):
                    copy.start()
            if (k, part, side) not in times:
                times[k, part, side] = copy
                sent.append((copy, to))

    def over(flow, k):
        return remote(
            passing.at[flow, k], passing.at[flow, k],
            r_send.at[flow, k], r_recv.at[flow, k], "over")

    def home(flow, k):
        size = parts[0][1]
        return remote(
            passing.at[flow, k], got.at[k, flow, pl.ds(0, size)],
            r_send.at[flow, k], t_recv.at[k, 0, flow], "end")

    def pass_on(made, one, other, picked):
        if not detour:
            return
        for k in picked:
            for there, flow in ((one, 0), (other, 1)):
                @pl.when(there)
                def _(flow=flow, k=k):
                    copy = made(flow, k)
                    over(flow, k).wait_recv()
                    copy.start()

    def stack(ref_value, size):
        v = ref_value.reshape(size * half, double)
        return jnp.concatenate([v[:, :c], v[:, c:]], axis=0)

    def own_part(k, part):
        at, size = parts[part]
        own = stack(mine[k, at:at + size], size)
        total = own.astype(F32) + mm(own, wtime[1])
        base[k, at:at + size] = total.reshape(size, columns, c)

    def skip_part(k, part):
        at, size = parts[part]
        total = base[k, at:at + size].reshape(size * columns, c)
        for side in range(2):
            landed(times[k, part, side], steps[side])
            total = total + mm(stack(got[k, side, at:at + size], size), wtime[2 * side])
        value = total.astype(BF16)
        n = size * half
        for j in range(size):
            s3[k, order[at + j] + 1, half:, :double] = jnp.concatenate(
                [value[j * half:(j + 1) * half], value[n + j * half:n + (j + 1) * half]], axis=1)

    edges = {}

    def share(k):
        pools = []
        for p in range(pooled_rows):
            pair = (s3[k, 2 * p + 1, half:, :double].astype(F32)
                    + s3[k, 2 * p + 2, half:, :double].astype(F32))
            pools.append(((pair[:, :c] + pair[:, c:]) * 0.25).astype(BF16))
        for side, (to, row, near) in enumerate((
            ("down", rows, pools[-2:]), ("up", 1, pools[:2]))):
            edge[k, side, 0] = s3[k, row, half:, :double]
            edge[k, side, 1] = jnp.concatenate(near, axis=1)
        for item in (1, 0):
            for side, to in enumerate(("down", "up")):
                copy = remote(
                    edge.at[k, side, item], edge_got.at[k, side, item],
                    e_send.at[k, side, item], e_recv.at[k, side, item], to)
                start(copy, to)
                edges[k, side, item] = copy
                sent.append((copy, to))
        for p in range(pooled_rows):
            spread(k, p + 2, pools[p])

    def spread(k, slot, pool):
        wide = pool.astype(F32)
        m3[k, slot] = jnp.concatenate(
            [later(wide).astype(BF16), pool, sooner(wide).astype(BF16)], axis=1)

    def turn_weights():
        for dr in range(3):
            turned = wup[dr].reshape(3 * c, -1).T
            wpool[dr] = turned[c:]
            for dw in range(3):
                wskip[dr, dw * c:(dw + 1) * c] = turned[:c, dw * c:(dw + 1) * c]

    def skip_weight(dr):
        return wskip[dr]

    wide = 2 * half

    def mid_weight(dr):
        return wmid[dr].reshape(3 * c, -1)

    def mid_inner(k):
        local = m3[k, 2:pooled_rows + 2].reshape(pooled_rows * half, 3 * c)
        mid_acc[k] = jnp.zeros(mid_acc.shape[1:], F32)
        for dr in range(3):
            term = mm(local, mid_weight(dr))
            mid_acc[k, 2 - dr:2 - dr + pooled_rows] += term.reshape(pooled_rows, half, -1)

    def up_first(k):
        n = rows - 2
        for r in range(1, rows - 1):
            widen(s3, k, r + 1)
        lhs = s3[k, 2:rows].reshape(n * wide, 3 * c)
        acc[k, 1:rows - 1] = mm(lhs, skip_weight(1)).reshape(n, wide, c)
        lower = mm(lhs, skip_weight(0)).reshape(n, wide, c)
        acc[k, rows - 1] = lower[n - 1]
        if n > 1:
            acc[k, 2:rows - 1] += lower[:n - 1]
        upper = mm(lhs, skip_weight(2)).reshape(n, wide, c)
        acc[k, 0] = upper[0]
        if n > 1:
            acc[k, 1:rows - 2] += upper[1:]

    def up_second(k):
        for r in (0, rows - 1):
            widen(s3, k, r + 1)
        lhs = jnp.concatenate([s3[k, 1], s3[k, rows]], axis=0)
        centre = mm(lhs, skip_weight(1))
        acc[k, 0] += centre[:wide]
        acc[k, rows - 1] += centre[wide:]
        acc[k, 1] += mm(s3[k, 1], skip_weight(0))
        acc[k, rows - 2] += mm(s3[k, rows], skip_weight(2))

    def finish(k):
        for side in range(2):
            landed(edges[k, side, 1], sources[side])
            both = edge_got[k, side, 1]
            first_slot = (0, pooled_rows + 2)[side]
            spread(k, first_slot, both[:, :c])
            spread(k, first_slot + 1, both[:, c:])
        n = pooled_rows + 2
        mid_acc[k, :2] += mm(
            m3[k, :2].reshape(2 * half, 3 * c), mid_weight(0)).reshape(2, half, -1)
        mid_acc[k, n - 2:] += mm(
            m3[k, n:].reshape(2 * half, 3 * c), mid_weight(2)).reshape(2, half, -1)
        term = mm(jnp.concatenate([m3[k, 1], m3[k, n]], axis=0), mid_weight(1))
        mid_acc[k, 0] += term[:half]
        mid_acc[k, n - 1] += term[half:]
        total = mid_acc[k]
        value = silu(total).astype(BF16)
        middle[k] = value
        @pl.when(jnp.logical_not(has["up"]))
        def _():
            middle[k, 0] = jnp.zeros(middle.shape[2:], BF16)
        @pl.when(jnp.logical_not(has["down"]))
        def _():
            middle[k, n - 1] = jnp.zeros(middle.shape[2:], BF16)
        for side in range(2):
            landed(edges[k, side, 0], sources[side])
            slot = (0, rows + 1)[side]
            s3[k, slot, half:, :double] = edge_got[k, side, 0]
            widen(s3, k, slot)
        acc[k, 0] += mm(s3[k, 0], skip_weight(0))
        acc[k, rows - 1] += mm(s3[k, rows + 1], skip_weight(2))
        spans = ((0, n - 1), (1, n - 2), (1, n - 1))
        terms = {}
        for dr, (at, size) in enumerate(spans):
            lhs = middle[k, at:at + size].reshape(size * half, -1)
            term = mm(lhs, wpool[dr])
            for j in range(size):
                terms[dr, at + j] = term[j * half:(j + 1) * half]
        for r in range(rows):
            taps = sum(terms[dr, (r + dr + 1) // 2] for dr in range(3))
            cols = [taps[:, dw * c:(dw + 1) * c] for dw in range(3)]
            even = later(cols[0]) + cols[1] + cols[2] + acc[k, r, :half]
            odd = cols[0] + cols[1] + sooner(cols[2]) + acc[k, r, half:]
            own = x3[k, r + 1, half:, :double].astype(F32)
            value = jnp.concatenate([even + own[:, :c], odd + own[:, c:]], axis=0).astype(BF16)
            out_hbm[k, r] = mm(value.T, split).astype(BF16)
        return None

    weights[0].wait()
    for k in range(clips):
        loads[k].wait()
        for r in range(rows):
            place(k, r + 1, raw[k, r])
        first_part(k, 0)
        send_part(k, 0, jnp.logical_not(jnp.logical_and(hops, outer)) if detour and k > 0 else None)
    pass_on(over, first_hop, last_hop, [0])
    for k in range(clips):
        for side in range(2):
            landed(halo[k, side], sources[side])
            place(k, (0, rows + 1)[side], raw_got[k, side])
        first_part(k, 1)
        if k == 0 and detour:
            pass_on(over, first_hop, last_hop, range(1, clips))
            for q in range(1, clips):
                send_part(q, 0, jnp.logical_and(hops, outer))
        if detour:
            send_part(k, 1, None, "far")
            if k == clips - 1:
                for q in range(clips):
                    send_part(q, 1, inside, "near")
        else:
            send_part(k, 1)
    for one in weights[1:]:
        one.wait()
    for k in range(clips):
        own_part(k, 0)
        own_part(k, 1)
    turn_weights()
    pass_on(home, last_hop, first_hop, range(clips))
    for k in range(clips):
        if detour:
            send_part(k, 1, outer, "near")
    for k in range(clips):
        skip_part(k, 0)
        up_first(k)
        skip_part(k, 1)
        share(k)
        if k > 0:
            finish(k - 1)
        mid_inner(k)
        up_second(k)
    finish(clips - 1)
    if detour:
        for flow in range(2):
            @pl.when(hops)
            def _(flow=flow):
                for k in range(clips):
                    over(flow, k).wait_send()
    for copy, to in sent:
        @pl.when(has[to])
        def _(copy=copy):
            copy.wait_send()


def body(count, latents, in_weight, time_weight, mid_weight, up_weight):
    clips, rows, columns, c = latents.shape
    cm = mid_weight.shape[-1]
    half, double = columns // 2, 2 * c
    flat = latents.swapaxes(2, 3)
    up_stored = up_weight.swapaxes(2, 3)
    dma = pltpu.SemaphoreType.DMA
    vmem = lambda *shape: pltpu.VMEM(shape, BF16)
    hbm = pl.BlockSpec(memory_space=pl.ANY)
    out = pl.pallas_call(
        functools.partial(kernel, count),
        out_shape=pltpu.VMEM(flat.shape, BF16),
        in_specs=[hbm] * 5,
        out_specs=pl.BlockSpec(memory_space=pltpu.VMEM),
        scratch_shapes=[
            vmem(clips, rows + 2, 2 * half, 3 * c),
            vmem(clips, rows + 2, 2 * half, 3 * c),
            vmem(clips, rows // 2 + 4, half, 3 * c),
            vmem(*in_weight.shape), vmem(*time_weight.shape),
            vmem(*mid_weight.shape), vmem(*up_stored.shape),
            vmem(3, 3 * c, c), vmem(3, cm, 3 * c),
            vmem(clips, rows, c, columns), vmem(clips, 2, c, columns),
            pltpu.VMEM((clips, rows, columns, c), F32),
            vmem(clips, rows, half, double),
            vmem(clips, 2, rows, half, double),
            vmem(clips, 2, 2, half, double),
            vmem(clips, 2, 2, half, double),
            vmem(clips, rows // 2 + 2, half, cm),
            pltpu.VMEM((clips, rows // 2 + 2, half, cm), F32),
            pltpu.VMEM((clips, rows, 2 * half, c), F32),
            vmem(clips, rows, c, columns), vmem(2, clips, rows - 2, half, double),
            dma((4,)), dma((clips,)), dma((clips,)),
            dma((clips, 2)), dma((clips, 2)),
            dma((clips, 2, 2)), dma((clips, 2, 2)),
            dma((clips, 2, 2)), dma((clips, 2, 2)),
            dma((2, clips)), dma((2, clips)),
        ],
        compiler_params=pltpu.CompilerParams(
            collective_id=0, has_side_effects=True, vmem_limit_bytes=50 * 1024 * 1024),
    )(*[pltpu.with_memory_space_constraint(v, pltpu.HBM) for v in (flat, in_weight, time_weight, mid_weight, up_stored)])
    return out.swapaxes(2, 3)


def solution(mesh):
    in_specs = (P("groups", "frames", None, None), P(), P(), P(), P())
    out_specs = P("groups", "frames", None, None)
    return jax.shard_map(
        functools.partial(body, mesh.shape["frames"]),
        mesh=mesh, in_specs=in_specs, out_specs=out_specs, check_vma=False)
```

```python
import functools

import jax
import jax.numpy as jnp
from jax import lax
from jax.experimental import pallas as pl
from jax.experimental.pallas import tpu as pltpu
from jax.sharding import PartitionSpec as P

FRAMES = 4
MESH = pl.DeviceIdType.MESH
F32 = jnp.float32
BF16 = jnp.bfloat16


def mm(a, b):
    return jnp.dot(a, b, preferred_element_type=F32)


def later(v):
    at = lax.broadcasted_iota(jnp.int32, v.shape, 0)
    return jnp.where(at == 0, 0.0, pltpu.roll(v, 1, 0))


def sooner(v):
    at = lax.broadcasted_iota(jnp.int32, v.shape, 0)
    return jnp.where(at == v.shape[0] - 1, 0.0, pltpu.roll(v, v.shape[0] - 1, 0))


def silu(v):
    return v / (1.0 + jnp.exp(-v))


def kernel(
    count, x_hbm, in_hbm, time_hbm, mid_hbm, up_hbm, out_hbm,
    x3, s3, m3, win, wtime, wmid, wup, wskip, wpool, raw, raw_got, base, mine, got, edge,
    edge_got, middle, mid_acc, acc, out_v, passing,
    w_sem, x_sem, o_sem, h_send, h_recv, t_send, t_recv, e_send, e_recv, r_send, r_recv,
):
    clips, rows, c, columns = x_hbm.shape
    half, double = columns // 2, 2 * c
    pooled_rows = rows // 2
    bands = count // FRAMES
    idx = lax.axis_index("frames")
    placed = lax.rem(idx + bands // 2, count)
    band = lax.rem(placed, bands)
    frame = placed // bands
    has = {
        "up": band > 0,
        "down": band < bands - 1,
        "prev": frame > 0,
        "next": frame < FRAMES - 1,
    }
    who = {
        "up": lax.rem(idx + count - 1, count),
        "down": lax.rem(idx + 1, count),
        "prev": lax.rem(idx + count - bands, count),
        "next": lax.rem(idx + bands, count),
    }

    reach = bands // 2
    detour = bands == 4
    ends = jnp.logical_and(frame < 2, band < reach)
    first_hop = jnp.logical_and(frame == FRAMES - 1, band >= reach)
    last_hop = jnp.logical_and(frame == 0, band >= reach)
    hops = jnp.logical_or(first_hop, last_hop)
    far_next = jnp.logical_and(frame == 0, band < reach)
    far_prev = jnp.logical_and(frame == 1, band < reach)
    greet = [(has[name], who[name]) for name in has]
    if detour:
        who["relay"] = lax.rem(idx + count - reach, count)
        who["end"] = lax.rem(idx + reach, count)
        who["over"] = jnp.where(
            first_hop, lax.rem(idx + 2 * reach, count), lax.rem(idx + count - 2 * reach, count))
        greet += [(ends, who["relay"]), (hops, who["end"]), (hops, who["over"])]

    def remote(src, dst, send, recv, name):
        return pltpu.make_async_remote_copy(
            src_ref=src, dst_ref=dst, send_sem=send, recv_sem=recv,
            device_id={"frames": who[name]}, device_id_type=MESH,
        )

    def start(copy, name):
        @pl.when(has[name])
        def _():
            copy.start()

    def landed(copy, name):
        @pl.when(has[name])
        def _():
            copy.wait_recv()

    sent = []

    loads = []
    for k in range(clips):
        loads.append(pltpu.make_async_copy(
            x_hbm.at[k], raw.at[k], x_sem.at[k]))
        loads[-1].start()
    weights = []
    for n, (src, dst) in enumerate(((in_hbm, win), (time_hbm, wtime), (mid_hbm, wmid), (up_hbm, wup))):
        weights.append(pltpu.make_async_copy(src, dst, w_sem.at[n]))
        weights[-1].start()

    barrier = pltpu.get_barrier_semaphore()
    for there, target in greet:
        @pl.when(there)
        def _(target=target):
            pl.semaphore_signal(
                barrier, inc=1, device_id={"frames": target}, device_id_type=MESH)
    pl.semaphore_wait(barrier, sum(there.astype(jnp.int32) for there, _ in greet))

    halo = {}
    for k in range(clips):
        for side, (to, row) in enumerate((("down", rows - 1), ("up", 0))):
            copy = remote(
                x_hbm.at[k, row], raw_got.at[k, side],
                h_send.at[k, side], h_recv.at[k, side], to)
            start(copy, to)
            halo[k, side] = copy
            sent.append((copy, to))
    sources = ("up", "down")
    steps = ("prev", "next")

    for side in range(2):
        @pl.when(jnp.logical_not(has[sources[side]]))
        def _(side=side):
            for k in range(clips):
                raw_got[k, side] = jnp.zeros((c, columns), BF16)
                edge_got[k, side] = jnp.zeros(edge_got.shape[2:], BF16)
        @pl.when(jnp.logical_not(has[steps[side]]))
        def _(side=side):
            for k in range(clips):
                got[k, side] = jnp.zeros(got.shape[2:], BF16)

    at = lax.broadcasted_iota(jnp.int32, (columns, columns), 0)
    to = lax.broadcasted_iota(jnp.int32, (columns, columns), 1)
    source = jnp.where(at < half, 2 * at, 2 * (at - half) + 1)
    split = jnp.where(to == source, 1.0, 0.0).astype(BF16)

    def place(k, slot, stored):
        value = lax.dot_general(
            split, stored, (((1,), (1,)), ((), ())), preferred_element_type=F32).astype(BF16)
        x3[k, slot, half:, :double] = jnp.concatenate([value[:half], value[half:]], axis=1)
        widen(x3, k, slot)

    def widen(dst, k, slot):
        row = dst[k, slot, half:, :double]
        even, odd = row[:, :c], row[:, c:]
        dst[k, slot, half:, double:] = sooner(even.astype(F32)).astype(BF16)
        dst[k, slot, :half, :] = jnp.concatenate(
            [later(odd.astype(F32)).astype(BF16), even, odd], axis=1)

    inner = list(range(1, rows - 1))
    order = inner + [0, rows - 1]
    parts = ((0, len(inner)), (len(inner), 2))

    def conv(src, k, picked, wref):
        total = None
        for dr in range(3):
            lhs = jnp.concatenate([src[k, r + dr] for r in picked], axis=0)
            term = mm(lhs, wref[dr].reshape(3 * c, c))
            total = term if total is None else total + term
        return total

    times = {}

    def first_part(k, part):
        at, size = parts[part]
        picked = order[at:at + size]
        value = silu(conv(x3, k, picked, win)).astype(BF16)
        for j in range(size):
            lo = 2 * half * j
            mine[k, at + j] = jnp.concatenate(
                [value[lo:lo + half], value[lo + half:lo + 2 * half]], axis=1)

    outer = jnp.logical_or(band == 0, band == bands - 1)
    inside = jnp.logical_not(outer)

    def send_part(k, part, now=None, way=None):
        at, size = parts[part]
        gate = lambda there: there if now is None else jnp.logical_and(there, now)
        for side, to in ((0, "next"), (1, "prev")):
            if way is not None:
                distant = (far_next, far_prev)[side]
                mask = distant if way == "far" else jnp.logical_not(distant)
                gate = lambda there, mask=mask: jnp.logical_and(
                    there if now is None else jnp.logical_and(there, now), mask)
            copy = remote(
                mine.at[k, pl.ds(at, size)], got.at[k, side, pl.ds(at, size)],
                t_send.at[k, part, side], t_recv.at[k, part, side], to)
            if detour and part == 0:
                far = (far_next, far_prev)[side]
                by = remote(
                    mine.at[k, pl.ds(at, size)], passing.at[side, k],
                    t_send.at[k, part, side], r_recv.at[side, k], "relay")
                @pl.when(gate(far))
                def _(by=by):
                    by.start()
                @pl.when(gate(jnp.logical_and(has[to], jnp.logical_not(far))))
                def _(copy=copy):
                    copy.start()
            else:
                @pl.when(gate(has[to]))
                def _(copy=copy):
                    copy.start()
            if (k, part, side) not in times:
                times[k, part, side] = copy
                sent.append((copy, to))

    def over(flow, k):
        return remote(
            passing.at[flow, k], passing.at[flow, k],
            r_send.at[flow, k], r_recv.at[flow, k], "over")

    def home(flow, k):
        size = parts[0][1]
        return remote(
            passing.at[flow, k], got.at[k, flow, pl.ds(0, size)],
            r_send.at[flow, k], t_recv.at[k, 0, flow], "end")

    def pass_on(made, one, other, picked):
        if not detour:
            return
        for k in picked:
            for there, flow in ((one, 0), (other, 1)):
                @pl.when(there)
                def _(flow=flow, k=k):
                    copy = made(flow, k)
                    over(flow, k).wait_recv()
                    copy.start()

    def stack(ref_value, size):
        v = ref_value.reshape(size * half, double)
        return jnp.concatenate([v[:, :c], v[:, c:]], axis=0)

    def own_part(k, part):
        at, size = parts[part]
        own = stack(mine[k, at:at + size], size)
        total = own.astype(F32) + mm(own, wtime[1])
        base[k, at:at + size] = total.reshape(size, columns, c)

    def skip_part(k, part):
        at, size = parts[part]
        total = base[k, at:at + size].reshape(size * columns, c)
        for side in range(2):
            landed(times[k, part, side], steps[side])
            total = total + mm(stack(got[k, side, at:at + size], size), wtime[2 * side])
        value = total.astype(BF16)
        n = size * half
        for j in range(size):
            s3[k, order[at + j] + 1, half:, :double] = jnp.concatenate(
                [value[j * half:(j + 1) * half], value[n + j * half:n + (j + 1) * half]], axis=1)

    edges = {}

    def share(k):
        pools = []
        for p in range(pooled_rows):
            pair = (s3[k, 2 * p + 1, half:, :double].astype(F32)
                    + s3[k, 2 * p + 2, half:, :double].astype(F32))
            pools.append(((pair[:, :c] + pair[:, c:]) * 0.25).astype(BF16))
        for side, (to, row, near) in enumerate((
            ("down", rows, pools[-2:]), ("up", 1, pools[:2]))):
            edge[k, side, 0] = s3[k, row, half:, :double]
            edge[k, side, 1] = jnp.concatenate(near, axis=1)
        for item in (1, 0):
            for side, to in enumerate(("down", "up")):
                copy = remote(
                    edge.at[k, side, item], edge_got.at[k, side, item],
                    e_send.at[k, side, item], e_recv.at[k, side, item], to)
                start(copy, to)
                edges[k, side, item] = copy
                sent.append((copy, to))
        for p in range(pooled_rows):
            spread(k, p + 2, pools[p])

    def spread(k, slot, pool):
        wide = pool.astype(F32)
        m3[k, slot] = jnp.concatenate(
            [later(wide).astype(BF16), pool, sooner(wide).astype(BF16)], axis=1)

    def turn_weights():
        for dr in range(3):
            turned = wup[dr].reshape(3 * c, -1).T
            wpool[dr] = turned[c:]
            for dw in range(3):
                wskip[dr, dw * c:(dw + 1) * c] = turned[:c, dw * c:(dw + 1) * c]

    def skip_weight(dr):
        return wskip[dr]

    wide = 2 * half

    def mid_weight(dr):
        return wmid[dr].reshape(3 * c, -1)

    def mid_inner(k):
        local = m3[k, 2:pooled_rows + 2].reshape(pooled_rows * half, 3 * c)
        mid_acc[k] = jnp.zeros(mid_acc.shape[1:], F32)
        for dr in range(3):
            term = mm(local, mid_weight(dr))
            mid_acc[k, 2 - dr:2 - dr + pooled_rows] += term.reshape(pooled_rows, half, -1)

    def up_first(k):
        n = rows - 2
        for r in range(1, rows - 1):
            widen(s3, k, r + 1)
        lhs = s3[k, 2:rows].reshape(n * wide, 3 * c)
        acc[k, 1:rows - 1] = mm(lhs, skip_weight(1)).reshape(n, wide, c)
        lower = mm(lhs, skip_weight(0)).reshape(n, wide, c)
        acc[k, rows - 1] = lower[n - 1]
        if n > 1:
            acc[k, 2:rows - 1] += lower[:n - 1]
        upper = mm(lhs, skip_weight(2)).reshape(n, wide, c)
        acc[k, 0] = upper[0]
        if n > 1:
            acc[k, 1:rows - 2] += upper[1:]

    def up_second(k):
        for r in (0, rows - 1):
            widen(s3, k, r + 1)
        lhs = jnp.concatenate([s3[k, 1], s3[k, rows]], axis=0)
        centre = mm(lhs, skip_weight(1))
        acc[k, 0] += centre[:wide]
        acc[k, rows - 1] += centre[wide:]
        acc[k, 1] += mm(s3[k, 1], skip_weight(0))
        acc[k, rows - 2] += mm(s3[k, rows], skip_weight(2))

    def finish(k):
        for side in range(2):
            landed(edges[k, side, 1], sources[side])
            both = edge_got[k, side, 1]
            first_slot = (0, pooled_rows + 2)[side]
            spread(k, first_slot, both[:, :c])
            spread(k, first_slot + 1, both[:, c:])
        n = pooled_rows + 2
        mid_acc[k, :2] += mm(
            m3[k, :2].reshape(2 * half, 3 * c), mid_weight(0)).reshape(2, half, -1)
        mid_acc[k, n - 2:] += mm(
            m3[k, n:].reshape(2 * half, 3 * c), mid_weight(2)).reshape(2, half, -1)
        term = mm(jnp.concatenate([m3[k, 1], m3[k, n]], axis=0), mid_weight(1))
        mid_acc[k, 0] += term[:half]
        mid_acc[k, n - 1] += term[half:]
        total = mid_acc[k]
        value = silu(total).astype(BF16)
        middle[k] = value
        @pl.when(jnp.logical_not(has["up"]))
        def _():
            middle[k, 0] = jnp.zeros(middle.shape[2:], BF16)
        @pl.when(jnp.logical_not(has["down"]))
        def _():
            middle[k, n - 1] = jnp.zeros(middle.shape[2:], BF16)
        for side in range(2):
            landed(edges[k, side, 0], sources[side])
            slot = (0, rows + 1)[side]
            s3[k, slot, half:, :double] = edge_got[k, side, 0]
            widen(s3, k, slot)
        acc[k, 0] += mm(s3[k, 0], skip_weight(0))
        acc[k, rows - 1] += mm(s3[k, rows + 1], skip_weight(2))
        spans = ((0, n - 1), (1, n - 2), (1, n - 1))
        terms = {}
        for dr, (at, size) in enumerate(spans):
            lhs = middle[k, at:at + size].reshape(size * half, -1)
            term = mm(lhs, wpool[dr])
            for j in range(size):
                terms[dr, at + j] = term[j * half:(j + 1) * half]
        for r in range(rows):
            taps = sum(terms[dr, (r + dr + 1) // 2] for dr in range(3))
            cols = [taps[:, dw * c:(dw + 1) * c] for dw in range(3)]
            even = later(cols[0]) + cols[1] + cols[2] + acc[k, r, :half]
            odd = cols[0] + cols[1] + sooner(cols[2]) + acc[k, r, half:]
            own = x3[k, r + 1, half:, :double].astype(F32)
            value = jnp.concatenate([even + own[:, :c], odd + own[:, c:]], axis=0).astype(BF16)
            out_hbm[k, r] = mm(value.T, split).astype(BF16)
        return None

    weights[0].wait()
    for k in range(clips):
        loads[k].wait()
        for r in range(rows):
            place(k, r + 1, raw[k, r])
        first_part(k, 0)
        send_part(k, 0)
    pass_on(over, first_hop, last_hop, [0])
    for k in range(clips):
        for side in range(2):
            landed(halo[k, side], sources[side])
            place(k, (0, rows + 1)[side], raw_got[k, side])
        first_part(k, 1)
        if k == 0 and detour:
            pass_on(over, first_hop, last_hop, range(1, clips))
        if detour:
            send_part(k, 1, None, "far")
            if k == clips - 1:
                for q in range(clips):
                    send_part(q, 1, inside, "near")
        else:
            send_part(k, 1)
    for one in weights[1:]:
        one.wait()
    for k in range(clips):
        own_part(k, 0)
        own_part(k, 1)
    turn_weights()
    pass_on(home, last_hop, first_hop, range(clips))
    for k in range(clips):
        if detour:
            send_part(k, 1, outer, "near")
    for k in range(clips):
        skip_part(k, 0)
        up_first(k)
        skip_part(k, 1)
        share(k)
        if k > 0:
            finish(k - 1)
        mid_inner(k)
        up_second(k)
    finish(clips - 1)
    if detour:
        for flow in range(2):
            @pl.when(hops)
            def _(flow=flow):
                for k in range(clips):
                    over(flow, k).wait_send()
    for copy, to in sent:
        @pl.when(has[to])
        def _(copy=copy):
            copy.wait_send()


def body(count, latents, in_weight, time_weight, mid_weight, up_weight):
    clips, rows, columns, c = latents.shape
    cm = mid_weight.shape[-1]
    half, double = columns // 2, 2 * c
    flat = latents.swapaxes(2, 3)
    up_stored = up_weight.swapaxes(2, 3)
    dma = pltpu.SemaphoreType.DMA
    vmem = lambda *shape: pltpu.VMEM(shape, BF16)
    hbm = pl.BlockSpec(memory_space=pl.ANY)
    out = pl.pallas_call(
        functools.partial(kernel, count),
        out_shape=pltpu.VMEM(flat.shape, BF16),
        in_specs=[hbm] * 5,
        out_specs=pl.BlockSpec(memory_space=pltpu.VMEM),
        scratch_shapes=[
            vmem(clips, rows + 2, 2 * half, 3 * c),
            vmem(clips, rows + 2, 2 * half, 3 * c),
            vmem(clips, rows // 2 + 4, half, 3 * c),
            vmem(*in_weight.shape), vmem(*time_weight.shape),
            vmem(*mid_weight.shape), vmem(*up_stored.shape),
            vmem(3, 3 * c, c), vmem(3, cm, 3 * c),
            vmem(clips, rows, c, columns), vmem(clips, 2, c, columns),
            pltpu.VMEM((clips, rows, columns, c), F32),
            vmem(clips, rows, half, double),
            vmem(clips, 2, rows, half, double),
            vmem(clips, 2, 2, half, double),
            vmem(clips, 2, 2, half, double),
            vmem(clips, rows // 2 + 2, half, cm),
            pltpu.VMEM((clips, rows // 2 + 2, half, cm), F32),
            pltpu.VMEM((clips, rows, 2 * half, c), F32),
            vmem(clips, rows, c, columns), vmem(2, clips, rows - 2, half, double),
            dma((4,)), dma((clips,)), dma((clips,)),
            dma((clips, 2)), dma((clips, 2)),
            dma((clips, 2, 2)), dma((clips, 2, 2)),
            dma((clips, 2, 2)), dma((clips, 2, 2)),
            dma((2, clips)), dma((2, clips)),
        ],
        compiler_params=pltpu.CompilerParams(
            collective_id=0, has_side_effects=True, vmem_limit_bytes=50 * 1024 * 1024),
    )(*[pltpu.with_memory_space_constraint(v, pltpu.HBM) for v in (flat, in_weight, time_weight, mid_weight, up_stored)])
    return out.swapaxes(2, 3)


def solution(mesh):
    in_specs = (P("groups", "frames", None, None), P(), P(), P(), P())
    out_specs = P("groups", "frames", None, None)
    return jax.shard_map(
        functools.partial(body, mesh.shape["frames"]),
        mesh=mesh, in_specs=in_specs, out_specs=out_specs, check_vma=False)
```
